32 devices in a mesh: parts: 2 (over y), rows: 4 (over z), ex: 4 (over x, core).
Axes of the slice: x: 2, y: 2, z: 4, core: 2. Of those that a mesh axis runs over, the one named last changes fastest.
Arguments:
- hidden_acts: bfloat16 [1024, 512], P(('parts', 'ex'), 'rows'), parts along dimension 0, may hold values from -6 to 6
- cotangent: bfloat16 [1024, 4096], P(('parts', 'ex'), 'rows'), parts along dimension 0, may hold values from -0.796875 to 0.796875
- lengths: int32 [64], P('parts'), parts along dimension 0, may hold values from 1 to 64, 512 in all
- row_signs: int32 [512], P('rows'), may hold values from -1 to 1, as said below
- col_signs: int32 [4096], replicated, may hold values from -1 to 1, as said below
- feat_row: int32 [8192], replicated, may hold values from 0 to 511
- feat_col: int32 [8192], replicated, may hold values from 0 to 4095
- inverse_rows: bfloat16 [8192, 8192], P('rows'), as said below
Outputs:
- scores: bfloat16 [64, 8192], P(('parts', 'ex'), 'rows'), parts along dimension 0
The draws below stay inside these ranges and needn't reach their ends.
There are 2 independent parts, one for each index of `parts`. The reference program is written for one: setup_inputs(seed, part) draws one part's arguments, and reference() takes and returns one part's arrays. A program takes and returns all parts, laid end to end along the dimension named above; an argument that names none is the same for every part. Nothing has to cross between parts.
Inputs may be any that keep to these rules, and one draw needn't show every extreme that they name: `row_signs`: every entry is -1 or +1. `col_signs`: every entry is -1 or +1. `inverse_rows`: the whole matrix equals its transpose. The lengths sum to 512 and the largest equals 64.
All inputs are finite; a program needn't handle non-finite values.
Results may differ from the reference program's by a relative error of at most 0.0049.
Values may be sent and summed in bfloat16 or wider, within the bound.
A program may use at most 128 MiB of HBM per device.

```python
import math
import jax
import jax.numpy as jnp
import numpy as np
from jax import lax

D = 4096
FFW_DEV = 128
FFW = 512
K = 8192
EXAMPLES = 32
TOKENS = 512
MOST = 64
N_ROWS = 4


def draw_row_signs(key, part):
    return (2 * jax.random.randint(key, (FFW,), 0, 2) - 1).astype(jnp.int32)


def draw_col_signs(key, part):
    return (2 * jax.random.randint(key, (D,), 0, 2) - 1).astype(jnp.int32)


def draw_inverse_rows(key, part):
    base = jax.random.normal(key, (K, K), jnp.float32)
    mixed = (base + base.T) / jnp.sqrt(2.0 * K)
    weight = 0.3
    return (jnp.eye(K, dtype=jnp.float32) + weight * mixed).astype(jnp.bfloat16)


def place_ends(values, stream_key, smallest, high):
    dims = values.shape
    spot = [jax.random.randint(jax.random.fold_in(stream_key, axis), (), 0, dims[axis]) for axis in range(len(dims))]
    values = values.at[tuple(spot)].set(smallest)
    longest = dims.index(max(dims))
    spot[longest] = (spot[longest] + 1) % dims[longest]
    return values.at[tuple(spot)].set(high)


def levels(key, extent, split, smallest, largest):
    level = 1.0
    for dim, shards_of in split:
        heights = jax.random.uniform(jax.random.fold_in(jax.random.fold_in(key, 6), dim), (shards_of,), jnp.float32, smallest / len(split), largest / len(split))
        level = level * jnp.repeat(jnp.exp(heights), extent[dim] // shards_of).reshape((-1,) + (1,) * (len(extent) - 1 - dim))
    return level


def split_up(number_of, total, most, lean):
    portions = [(1 << 20) // math.isqrt(standing ** lean) + 1 for standing in range(2, number_of + 1)]
    rest, counts = total - most - (number_of - 1), [1] * (number_of - 1)
    while rest > 0:
        free = [i for i in range(number_of - 1) if counts[i] < most]
        pool, left = sum([portions[i] for i in free]), rest
        for i in free:
            more = min(most - counts[i], max(1, left * portions[i] // pool), rest)
            counts[i] = counts[i] + more
            rest = rest - more
    return np.array([most] + counts)


def ragged_sizes(own_key, number_of, total, most, lean):
    if number_of == 2:
        one = jax.random.randint(own_key, (), max(1, total - most), min(most, total - 1) + 1)
        return jnp.stack([one, total - one])
    sizes = jnp.asarray(split_up(number_of, total, most, lean), jnp.int32)
    twos = (number_of - 1) // 2
    source_of, sink = sizes[1:1 + 2 * twos:2], sizes[2:2 + 2 * twos:2]
    room = jnp.minimum(source_of - 1, most - sink)
    shifted = jax.random.randint(jax.random.fold_in(own_key, 1), (twos,), 0, 1 << 20) % (room + 1)
    sizes = sizes.at[1:1 + 2 * twos:2].set(source_of - shifted).at[2:2 + 2 * twos:2].set(sink + shifted)
    return sizes[jax.random.permutation(jax.random.fold_in(own_key, 2), number_of)]


def normal_values(rng, shape, width, limit, pieces=(), kind=jnp.bfloat16):
    result = jax.random.normal(rng, shape, jnp.float32) * width
    if len(pieces) > 0:
        result = levels(rng, shape, pieces, -0.22, 0.18) * result
    return jnp.clip(result, min=-limit, max=limit).astype(kind)


def setup_inputs(seed: int = 0, part: int = 0) -> dict:
    key_of = jax.random.split(jax.random.key(seed), 9)
    part_keys = jax.random.split(jax.random.fold_in(key_of[8], part), 9)
    hidden_acts = normal_values(part_keys[0], (TOKENS, FFW), 1.0, 6.0, ((0, 4), (1, 4)))
    cotangent = normal_values(part_keys[1], (TOKENS, D), 0.1, 0.796875, ((0, 4), (1, 4)))
    lengths = ragged_sizes(part_keys[2], EXAMPLES, TOKENS, MOST, 2).astype(jnp.int32)
    row_signs = draw_row_signs(jax.random.fold_in(key_of[8], 71), part)
    col_signs = draw_col_signs(jax.random.fold_in(key_of[8], 71), part)
    feat_row = place_ends(jax.random.randint(key_of[5], (K,), 0, FFW), jax.random.fold_in(key_of[5], 1), 0, FFW - 1).astype(jnp.int32)
    feat_col = place_ends(jax.random.randint(key_of[6], (K,), 0, D), jax.random.fold_in(key_of[6], 1), 0, D - 1).astype(jnp.int32)
    inverse_rows = draw_inverse_rows(jax.random.fold_in(key_of[8], 71), part)
    return {"hidden_acts": hidden_acts, "cotangent": cotangent, "lengths": lengths, "row_signs": row_signs, "col_signs": col_signs, "feat_row": feat_row, "feat_col": feat_col, "inverse_rows": inverse_rows}


def hadamard(mat_size):
    indices = jnp.arange(mat_size, dtype=jnp.int32)
    common = indices[:, None] & indices[None, :]
    parity = jnp.zeros((mat_size, mat_size), jnp.int32)
    for bit_pos in range(max(mat_size.bit_length() - 1, 0)):
        parity = parity + (common >> bit_pos & 1)
    return (1 - 2 * (parity % 2)).astype(jnp.float32)

def kron_apply(values, outer_mat, inner_mat):
    tokens = values.shape[0]
    shaped = values.reshape(tokens, outer_mat.shape[0], inner_mat.shape[0])
    shaped = jnp.einsum('tri,ia->tra', shaped, inner_mat, precision=lax.Precision.HIGHEST)
    shaped = jnp.einsum('tra,rh->tha', shaped, outer_mat, precision=lax.Precision.HIGHEST)
    return shaped.reshape(tokens, -1)

def reference(hidden_acts, cotangent, lengths, row_signs, col_signs, feat_row, feat_col, inverse_rows):
    left_side = hidden_acts.astype(jnp.float32) * row_signs.astype(jnp.float32)[None, :]
    left_side = kron_apply(left_side, hadamard(N_ROWS), hadamard(FFW_DEV))
    inner_width = min(D, 128)
    right_side = cotangent.astype(jnp.float32) * col_signs.astype(jnp.float32)[None, :]
    right_side = kron_apply(right_side, hadamard(D // inner_width), hadamard(inner_width))
    ex_end = jnp.cumsum(lengths).astype(jnp.int32)
    positions = jnp.arange(TOKENS, dtype=jnp.int32)
    owner = lax.optimization_barrier(jnp.sum((positions[:, None] >= ex_end[None, :]).astype(jnp.int32), axis=1))
    member = (owner[:, None] == jnp.arange(EXAMPLES, dtype=jnp.int32)[None, :]).astype(jnp.float32)
    picked = jnp.take(left_side, feat_row, axis=1) * jnp.take(right_side, feat_col, axis=1)
    features = jnp.dot(member.T, picked, precision=lax.Precision.HIGHEST) * (1.0 / math.sqrt(FFW * D))
    features_low = features.astype(jnp.bfloat16)
    return jnp.dot(features_low, inverse_rows, preferred_element_type=jnp.float32).astype(jnp.bfloat16)
```

```python
import functools
import math

import jax
import jax.numpy as jnp
from jax import lax
from jax.experimental import pallas as pl
from jax.experimental.pallas import tpu as pltpu
from jax.sharding import PartitionSpec as P


def signs(first_bits, second_bits):
    odd = lax.population_count(first_bits & second_bits) & 1
    return (1 - 2 * odd).astype(jnp.float32).astype(jnp.bfloat16)


def sign_rows(first, count, step, picks):
    inner = lax.broadcasted_iota(jnp.int32, (step, picks.shape[1]), 0)
    table = signs(inner, picks)
    parts = [table * signs(jnp.zeros_like(picks) + (first + n * step), picks) for n in range(count)]
    return parts[0] if count == 1 else jnp.concatenate(parts, axis=0)


def loop(count, body):
    if count <= 4:
        for n in range(count):
            body(n)
    else:
        lax.fori_loop(0, count, lambda n, c: (body(n), c)[1], 0)


def when(cond, body):
    if isinstance(cond, bool):
        if cond:
            body()
    else:
        pl.when(cond)(body)


def kernel(
    row_count,
    ex_count,
    norm_scale,
    hid_ref,
    cot_ref,
    len_ref,
    rsign_ref,
    csign_ref,
    frow_ref,
    fcol_ref,
    inv_ref,
    out_ref,
    hid_all,
    cot_signed,
    right_buf,
    part_buf,
    ex_in,
    row_in,
    low_all,
    inv_buf,
    total_buf,
    inv_sem,
    hid_send,
    hid_recv,
    ex_send,
    ex_recv,
    row_send,
    row_recv,
    low_send,
    low_recv,
):
    row = lax.axis_index("rows")
    ex = lax.axis_index("ex")
    tok_dev, width = hid_ref.shape
    cot_width = cot_ref.shape[1]
    features = frow_ref.shape[1]
    own = features // row_count
    examples = len_ref.shape[1]
    chunk = min(own, 512)
    ex_steps = ex_count.bit_length() - 1

    def inv_copy(n):
        q = lax.rem(row + n, row_count)
        cols = pl.ds(pl.multiple_of(q * own, 128), own)
        return pltpu.make_async_copy(inv_ref.at[:, cols], inv_buf.at[q], inv_sem.at[q])

    barrier = pltpu.get_barrier_semaphore()

    def greet(n):
        pl.semaphore_signal(
            barrier,
            inc=1,
            device_id={"rows": lax.rem(row + n + 1, row_count)},
            device_id_type=pl.DeviceIdType.MESH,
        )

    loop(row_count - 1, greet)

    def bit_of(step):
        return lax.rem(ex // (1 << step), 2)

    def partner_of(step):
        return ex + (1 - 2 * bit_of(step)) * (1 << step)

    for step in range(ex_steps):
        pl.semaphore_signal(
            barrier,
            inc=1,
            device_id={"ex": partner_of(step)},
            device_id_type=pl.DeviceIdType.MESH,
        )
    loop(row_count, lambda n: inv_copy(n).start())
    hid_all[row] = hid_ref[...] * rsign_ref[...].astype(jnp.float32).astype(jnp.bfloat16)
    if csign_ref.shape[1] == cot_width:
        col_sign = csign_ref[...]
    else:
        col_sign = csign_ref[:, pl.ds(pl.multiple_of(row * cot_width, 128), cot_width)]
    cot_signed[...] = cot_ref[...] * col_sign.astype(jnp.float32).astype(jnp.bfloat16)
    lens = jnp.broadcast_to(len_ref[...].astype(jnp.float32), (examples, examples))
    e_row = lax.broadcasted_iota(jnp.int32, (examples, examples), 0)
    e_col = lax.broadcasted_iota(jnp.int32, (examples, examples), 1)
    ends = jnp.sum(jnp.where(e_col <= e_row, lens, 0.0), axis=1, keepdims=True)
    starts = jnp.sum(jnp.where(e_col < e_row, lens, 0.0), axis=1, keepdims=True)
    spots = ex * tok_dev + lax.broadcasted_iota(jnp.int32, (examples, tok_dev), 1)
    spots = spots.astype(jnp.float32)
    member = jnp.where((spots >= starts) & (spots < ends), 1.0, 0.0).astype(jnp.bfloat16)
    pl.semaphore_wait(barrier, row_count - 1 + ex_steps)

    def hid_copy(n, incoming=False):
        to = lax.rem(row + n + 1, row_count)
        block = lax.rem(row - n - 1 + row_count, row_count) if incoming else row
        return pltpu.make_async_remote_copy(
            src_ref=hid_all.at[block],
            dst_ref=hid_all.at[block],
            send_sem=hid_send.at[n],
            recv_sem=hid_recv.at[n],
            device_id={"rows": to},
            device_id_type=pl.DeviceIdType.MESH,
        )

    loop(row_count - 1, lambda n: hid_copy(n).start())

    def block_of(i):
        return lax.rem(row + 1 + i, row_count)

    def picks_of(ref, i, c):
        at = pl.multiple_of(block_of(i) * own + c * chunk, 128)
        return ref[:, pl.ds(at, chunk)]

    inner = min(cot_width, 128)

    def right_side(i):
        def one(c):
            table = sign_rows(row * cot_width, cot_width // inner, inner, picks_of(fcol_ref, i, c))
            at = c * chunk if isinstance(c, int) else pl.multiple_of(c * chunk, 128)
            right_buf[i, :, pl.ds(at, chunk)] = jnp.dot(
                cot_signed[...], table, preferred_element_type=jnp.float32
            )

        loop(own // chunk, one)

    group = min(row_count, 4)

    def features_of(i):
        def one(c):
            picks = picks_of(frow_ref, i, c)

            def some(g, left):
                acts = jnp.concatenate([hid_all[g * group + n] for n in range(group)], axis=1)
                table = sign_rows(g * group * width, group, width, picks)
                return left + jnp.dot(acts, table, preferred_element_type=jnp.float32)

            left = jnp.zeros((tok_dev, chunk), jnp.float32)
            if row_count == group:
                left = some(0, left)
            else:
                left = lax.fori_loop(0, row_count // group, some, left)
            at = c * chunk if isinstance(c, int) else pl.multiple_of(c * chunk, 128)
            products = left * right_buf[i, :, pl.ds(at, chunk)]
            high = products.astype(jnp.bfloat16)
            rest = (products - high.astype(jnp.float32)).astype(jnp.bfloat16)
            sums = jnp.dot(member, high, preferred_element_type=jnp.float32)
            sums = sums + jnp.dot(member, rest, preferred_element_type=jnp.float32)
            part_buf[i, :, :, pl.ds(at, chunk)] = sums.reshape(ex_count, examples // ex_count, chunk)

        loop(own // chunk, one)

    def ex_copies(i, step):
        size = 1 << step
        first = ex_count - (ex_count >> step)
        copies = []
        for m in range(ex_count >> (step + 1)):
            away = lax.rem(ex, size) + (1 - bit_of(step)) * size + m * 2 * size
            slot = first + m
            copies.append(
                pltpu.make_async_remote_copy(
                    src_ref=part_buf.at[i, away],
                    dst_ref=ex_in.at[i, slot],
                    send_sem=ex_send.at[i, slot],
                    recv_sem=ex_recv.at[i, slot],
                    device_id={"ex": partner_of(step)},
                    device_id_type=pl.DeviceIdType.MESH,
                )
            )
        return copies

    def ex_start(i, step):
        for copy in ex_copies(i, step):
            copy.start()

    def ex_finish(i, step):
        size = 1 << step
        first = ex_count - (ex_count >> step)
        for m, copy in enumerate(ex_copies(i, step)):
            copy.wait_recv()
            mine = lax.rem(ex, 2 * size) + m * 2 * size
            part_buf[i, mine] = part_buf[i, mine] + ex_in[i, first + m]

    def row_copy(i):
        return pltpu.make_async_remote_copy(
            src_ref=part_buf.at[i, ex],
            dst_ref=row_in.at[i],
            send_sem=row_send.at[i],
            recv_sem=row_recv.at[i],
            device_id={"rows": block_of(i)},
            device_id_type=pl.DeviceIdType.MESH,
        )

    def stage(i, step):
        def work():
            if step > 0:
                ex_finish(i, step - 1)
            if step < ex_steps:
                ex_start(i, step)
            else:
                when(i < row_count - 1, lambda: row_copy(i).start())

        return work

    right_side(0)
    if row_count > 1:
        right_side(1)
    loop(row_count - 1, lambda n: hid_copy(n, True).wait_recv())

    def block_step(i):
        features_of(i)
        stage(i, 0)()
        for step in range(1, ex_steps + 1):
            when(i >= step, stage(i - step, step))
        when(i + 2 < row_count, lambda: right_side(i + 2))

    loop(row_count, block_step)
    for late in range(1, ex_steps + 1):
        for step in range(late, ex_steps + 1):
            if row_count - 1 + late - step >= 0:
                stage(row_count - 1 + late - step, step)()

    total_buf[...] = part_buf[row_count - 1, ex]

    def add_row(n):
        row_copy(n).wait_recv()
        total_buf[...] = total_buf[...] + row_in[n]

    loop(row_count - 1, add_row)
    low_all[row] = (total_buf[...] * norm_scale).astype(jnp.bfloat16)

    def low_copy(n, incoming=False):
        block = lax.rem(row - n - 1 + row_count, row_count) if incoming else row
        return pltpu.make_async_remote_copy(
            src_ref=low_all.at[block],
            dst_ref=low_all.at[block],
            send_sem=low_send.at[n],
            recv_sem=low_recv.at[n],
            device_id={"rows": lax.rem(row + n + 1, row_count)},
            device_id_type=pl.DeviceIdType.MESH,
        )

    loop(row_count - 1, lambda n: low_copy(n).start())
    tile = min(own, 256)

    def score_block(n):
        q = lax.rem(row - n + row_count, row_count)
        when(n > 0, lambda: low_copy(n - 1, True).wait_recv())
        pltpu.make_async_copy(
            inv_ref.at[:, pl.ds(pl.multiple_of(q * own, 128), own)], inv_buf.at[q], inv_sem.at[q]
        ).wait()
        low = low_all[q]

        def one(j, carry):
            at = pl.multiple_of(j * tile, 128)
            got = lax.dot_general(
                low,
                inv_buf[q, pl.ds(at, tile), :],
                (((1,), (1,)), ((), ())),
                preferred_element_type=jnp.float32,
            )
            before = jnp.where(n > 0, total_buf[:, pl.ds(at, tile)], 0.0)
            total_buf[:, pl.ds(at, tile)] = before + got
            return carry

        lax.fori_loop(0, own // tile, one, 0)

    loop(row_count, score_block)
    out_ref[...] = total_buf[...].astype(out_ref.dtype)
    loop(row_count - 1, lambda n: hid_copy(n).wait_send())
    loop(row_count - 1, lambda n: low_copy(n).wait_send())
    loop(row_count - 1, lambda n: row_copy(n).wait_send())

    def ex_sent(i):
        for step in range(ex_steps):
            for copy in ex_copies(i, step):
                copy.wait_send()

    loop(row_count, ex_sent)


def local(hidden_acts, cotangent, lengths, row_signs, col_signs, feat_row, feat_col, inverse_rows):
    row_count = lax.axis_size("rows")
    ex_count = lax.axis_size("ex")
    tok_dev, width = hidden_acts.shape
    cot_width = cotangent.shape[1]
    features = feat_row.shape[0]
    examples = lengths.shape[0]
    own = features // row_count
    owned = examples // ex_count
    norm_scale = 1.0 / math.sqrt(width * row_count * col_signs.shape[0])
    if cot_width % 128 != 0:
        col_signs = lax.dynamic_slice(col_signs, (lax.axis_index("rows") * cot_width,), (cot_width,))
    vmem = pl.BlockSpec(memory_space=pltpu.VMEM)
    others = max(row_count - 1, 1)
    dma = pltpu.SemaphoreType.DMA
    return pl.pallas_call(
        functools.partial(kernel, row_count, ex_count, norm_scale),
        out_shape=jax.ShapeDtypeStruct((owned, own), jnp.bfloat16),
        in_specs=[vmem] * 7 + [pl.BlockSpec(memory_space=pl.ANY)],
        out_specs=vmem,
        scratch_shapes=[
            pltpu.VMEM((row_count, tok_dev, width), jnp.bfloat16),
            pltpu.VMEM((tok_dev, cot_width), jnp.bfloat16),
            pltpu.VMEM((row_count, tok_dev, own), jnp.float32),
            pltpu.VMEM((row_count, ex_count, owned, own), jnp.float32),
            pltpu.VMEM((row_count, max(ex_count - 1, 1), owned, own), jnp.float32),
            pltpu.VMEM((others, owned, own), jnp.float32),
            pltpu.VMEM((row_count, owned, own), jnp.bfloat16),
            pltpu.VMEM((row_count, own, own), jnp.bfloat16),
            pltpu.VMEM((owned, own), jnp.float32),
            dma((row_count,)),
            dma((others,)),
            dma((others,)),
            dma((row_count, max(ex_count - 1, 1))),
            dma((row_count, max(ex_count - 1, 1))),
            dma((others,)),
            dma((others,)),
            dma((others,)),
            dma((others,)),
        ],
        compiler_params=pltpu.CompilerParams(
            collective_id=0, has_side_effects=True, vmem_limit_bytes=60 * 1024 * 1024
        ),
        name="features_and_scores",
    )(
        hidden_acts,
        cotangent,
        lengths.reshape(1, -1),
        row_signs.reshape(1, -1),
        col_signs.reshape(1, -1),
        feat_row.reshape(1, -1),
        feat_col.reshape(1, -1),
        inverse_rows,
    )


def solution(mesh):
    placed = (
        P(("parts", "ex"), "rows"),
        P(("parts", "ex"), "rows"),
        P("parts"),
        P("rows"),
        P(),
        P(),
        P(),
        P("rows", None),
    )
    return jax.shard_map(
        local, mesh=mesh, in_specs=placed, out_specs=P(("parts", "ex"), "rows"), check_vma=False
    )
```

```python
import functools
import math

import jax
import jax.numpy as jnp
from jax import lax
from jax.experimental import pallas as pl
from jax.experimental.pallas import tpu as pltpu
from jax.sharding import PartitionSpec as P


def signs(first_bits, second_bits):
    odd = lax.population_count(first_bits & second_bits) & 1
    return (1 - 2 * odd).astype(jnp.float32).astype(jnp.bfloat16)


def sign_rows(first, count, step, picks):
    inner = lax.broadcasted_iota(jnp.int32, (step, picks.shape[1]), 0)
    table = signs(inner, picks)
    parts = [table * signs(jnp.zeros_like(picks) + (first + n * step), picks) for n in range(count)]
    return parts[0] if count == 1 else jnp.concatenate(parts, axis=0)


def loop(count, body):
    if count <= 4:
        for n in range(count):
            body(n)
    else:
        lax.fori_loop(0, count, lambda n, c: (body(n), c)[1], 0)


def when(cond, body):
    if isinstance(cond, bool):
        if cond:
            body()
    else:
        pl.when(cond)(body)


def kernel(
    row_count,
    ex_count,
    norm_scale,
    hid_ref,
    cot_ref,
    len_ref,
    rsign_ref,
    csign_ref,
    frow_ref,
    fcol_ref,
    inv_ref,
    out_ref,
    hid_all,
    cot_signed,
    right_buf,
    part_buf,
    ex_in,
    row_in,
    score_out,
    score_in,
    inv_buf,
    total_buf,
    inv_sem,
    hid_send,
    hid_recv,
    ex_send,
    ex_recv,
    row_send,
    row_recv,
    score_send,
    score_recv,
):
    row = lax.axis_index("rows")
    ex = lax.axis_index("ex")
    tok_dev, width = hid_ref.shape
    cot_width = cot_ref.shape[1]
    features = frow_ref.shape[1]
    own = features // row_count
    examples = len_ref.shape[1]
    chunk = min(own, 512)
    ex_steps = ex_count.bit_length() - 1

    def block_of(i):
        return lax.rem(row + 1 + i, row_count)

    def inv_copy(n):
        cols = pl.ds(pl.multiple_of(block_of(n) * own, 128), own)
        return pltpu.make_async_copy(inv_ref.at[:, cols], inv_buf.at[n], inv_sem.at[n])

    barrier = pltpu.get_barrier_semaphore()

    def greet(n):
        pl.semaphore_signal(
            barrier,
            inc=1,
            device_id={"rows": lax.rem(row + n + 1, row_count)},
            device_id_type=pl.DeviceIdType.MESH,
        )

    loop(row_count - 1, greet)

    def bit_of(step):
        return lax.rem(ex // (1 << step), 2)

    def partner_of(step):
        return ex + (1 - 2 * bit_of(step)) * (1 << step)

    for step in range(ex_steps):
        pl.semaphore_signal(
            barrier,
            inc=1,
            device_id={"ex": partner_of(step)},
            device_id_type=pl.DeviceIdType.MESH,
        )
    loop(row_count, lambda n: inv_copy(n).start())
    hid_all[row] = hid_ref[...] * rsign_ref[...].astype(jnp.float32).astype(jnp.bfloat16)
    if csign_ref.shape[1] == cot_width:
        col_sign = csign_ref[...]
    else:
        col_sign = csign_ref[:, pl.ds(pl.multiple_of(row * cot_width, 128), cot_width)]
    cot_signed[...] = cot_ref[...] * col_sign.astype(jnp.float32).astype(jnp.bfloat16)
    lens = jnp.broadcast_to(len_ref[...].astype(jnp.float32), (examples, examples))
    e_row = lax.broadcasted_iota(jnp.int32, (examples, examples), 0)
    e_col = lax.broadcasted_iota(jnp.int32, (examples, examples), 1)
    ends = jnp.sum(jnp.where(e_col <= e_row, lens, 0.0), axis=1, keepdims=True)
    starts = jnp.sum(jnp.where(e_col < e_row, lens, 0.0), axis=1, keepdims=True)
    spots = ex * tok_dev + lax.broadcasted_iota(jnp.int32, (examples, tok_dev), 1)
    spots = spots.astype(jnp.float32)
    member = jnp.where((spots >= starts) & (spots < ends), 1.0, 0.0).astype(jnp.bfloat16)
    pl.semaphore_wait(barrier, row_count - 1 + ex_steps)

    def hid_copy(n, incoming=False):
        to = lax.rem(row + n + 1, row_count)
        block = lax.rem(row - n - 1 + row_count, row_count) if incoming else row
        return pltpu.make_async_remote_copy(
            src_ref=hid_all.at[block],
            dst_ref=hid_all.at[block],
            send_sem=hid_send.at[n],
            recv_sem=hid_recv.at[n],
            device_id={"rows": to},
            device_id_type=pl.DeviceIdType.MESH,
        )

    loop(row_count - 1, lambda n: hid_copy(n).start())

    def picks_of(ref, i, c):
        at = pl.multiple_of(block_of(i) * own + c * chunk, 128)
        return ref[:, pl.ds(at, chunk)]

    inner = min(cot_width, 128)

    def right_side(i):
        def one(c):
            table = sign_rows(row * cot_width, cot_width // inner, inner, picks_of(fcol_ref, i, c))
            at = c * chunk if isinstance(c, int) else pl.multiple_of(c * chunk, 128)
            right_buf[i, :, pl.ds(at, chunk)] = jnp.dot(
                cot_signed[...], table, preferred_element_type=jnp.float32
            )

        loop(own // chunk, one)

    group = min(row_count, 4)

    def features_of(i):
        def one(c):
            picks = picks_of(frow_ref, i, c)

            def some(g, left):
                acts = jnp.concatenate([hid_all[g * group + n] for n in range(group)], axis=1)
                table = sign_rows(g * group * width, group, width, picks)
                return left + jnp.dot(acts, table, preferred_element_type=jnp.float32)

            left = jnp.zeros((tok_dev, chunk), jnp.float32)
            if row_count == group:
                left = some(0, left)
            else:
                left = lax.fori_loop(0, row_count // group, some, left)
            at = c * chunk if isinstance(c, int) else pl.multiple_of(c * chunk, 128)
            products = left * right_buf[i, :, pl.ds(at, chunk)]
            high = products.astype(jnp.bfloat16)
            rest = (products - high.astype(jnp.float32)).astype(jnp.bfloat16)
            sums = jnp.dot(member, high, preferred_element_type=jnp.float32)
            sums = sums + jnp.dot(member, rest, preferred_element_type=jnp.float32)
            part_buf[i, :, :, pl.ds(at, chunk)] = sums.reshape(ex_count, examples // ex_count, chunk)

        loop(own // chunk, one)

    def ex_copies(i, step):
        size = 1 << step
        first = ex_count - (ex_count >> step)
        copies = []
        for m in range(ex_count >> (step + 1)):
            away = lax.rem(ex, size) + (1 - bit_of(step)) * size + m * 2 * size
            slot = first + m
            copies.append(
                pltpu.make_async_remote_copy(
                    src_ref=part_buf.at[i, away],
                    dst_ref=ex_in.at[i, slot],
                    send_sem=ex_send.at[i, slot],
                    recv_sem=ex_recv.at[i, slot],
                    device_id={"ex": partner_of(step)},
                    device_id_type=pl.DeviceIdType.MESH,
                )
            )
        return copies

    def ex_start(i, step):
        for copy in ex_copies(i, step):
            copy.start()

    def ex_finish(i, step):
        size = 1 << step
        first = ex_count - (ex_count >> step)
        for m, copy in enumerate(ex_copies(i, step)):
            copy.wait_recv()
            mine = lax.rem(ex, 2 * size) + m * 2 * size
            part_buf[i, mine] = part_buf[i, mine] + ex_in[i, first + m]

    def row_copy(i):
        return pltpu.make_async_remote_copy(
            src_ref=part_buf.at[i, ex],
            dst_ref=row_in.at[i],
            send_sem=row_send.at[i],
            recv_sem=row_recv.at[i],
            device_id={"rows": block_of(i)},
            device_id_type=pl.DeviceIdType.MESH,
        )

    def stage(i, step):
        def work():
            if step > 0:
                ex_finish(i, step - 1)
            if step < ex_steps:
                ex_start(i, step)
            else:
                when(i < row_count - 1, lambda: row_copy(i).start())

        return work

    loop(row_count, right_side)
    loop(row_count - 1, lambda n: hid_copy(n, True).wait_recv())

    def block_step(i):
        features_of(i)
        stage(i, 0)()
        for step in range(1, ex_steps + 1):
            when(i >= step, stage(i - step, step))

    loop(row_count, block_step)
    for late in range(1, ex_steps + 1):
        for step in range(late, ex_steps + 1):
            if row_count - 1 + late - step >= 0:
                stage(row_count - 1 + late - step, step)()

    total_buf[...] = part_buf[row_count - 1, ex]

    def add_row(n):
        row_copy(n).wait_recv()
        total_buf[...] = total_buf[...] + row_in[n]

    loop(row_count - 1, add_row)
    low = (total_buf[...] * norm_scale).astype(jnp.bfloat16)

    def score_copy(n):
        return pltpu.make_async_remote_copy(
            src_ref=score_out.at[n],
            dst_ref=score_in.at[n],
            send_sem=score_send.at[n],
            recv_sem=score_recv.at[n],
            device_id={"rows": block_of(n)},
            device_id_type=pl.DeviceIdType.MESH,
        )

    tile = min(own, 512)

    def score_block(n):
        inv_copy(n).wait()

        def one(j):
            at = j * tile if isinstance(j, int) else pl.multiple_of(j * tile, 128)
            score_out[n, :, pl.ds(at, tile)] = jnp.dot(
                low, inv_buf[n, :, pl.ds(at, tile)], preferred_element_type=jnp.float32
            )

        loop(own // tile, one)
        when(n < row_count - 1, lambda: score_copy(n).start())

    loop(row_count, score_block)
    total_buf[...] = score_out[row_count - 1]

    def add_score(n):
        score_copy(n).wait_recv()
        total_buf[...] = total_buf[...] + score_in[n]

    loop(row_count - 1, add_score)
    out_ref[...] = total_buf[...].astype(out_ref.dtype)
    loop(row_count - 1, lambda n: hid_copy(n).wait_send())
    loop(row_count - 1, lambda n: score_copy(n).wait_send())
    loop(row_count - 1, lambda n: row_copy(n).wait_send())

    def ex_sent(i):
        for step in range(ex_steps):
            for copy in ex_copies(i, step):
                copy.wait_send()

    loop(row_count, ex_sent)


def local(hidden_acts, cotangent, lengths, row_signs, col_signs, feat_row, feat_col, inverse_rows):
    row_count = lax.axis_size("rows")
    ex_count = lax.axis_size("ex")
    tok_dev, width = hidden_acts.shape
    cot_width = cotangent.shape[1]
    features = feat_row.shape[0]
    examples = lengths.shape[0]
    own = features // row_count
    owned = examples // ex_count
    norm_scale = 1.0 / math.sqrt(width * row_count * col_signs.shape[0])
    if cot_width % 128 != 0:
        col_signs = lax.dynamic_slice(col_signs, (lax.axis_index("rows") * cot_width,), (cot_width,))
    vmem = pl.BlockSpec(memory_space=pltpu.VMEM)
    others = max(row_count - 1, 1)
    dma = pltpu.SemaphoreType.DMA
    return pl.pallas_call(
        functools.partial(kernel, row_count, ex_count, norm_scale),
        out_shape=jax.ShapeDtypeStruct((owned, own), jnp.bfloat16),
        in_specs=[vmem] * 7 + [pl.BlockSpec(memory_space=pl.ANY)],
        out_specs=vmem,
        scratch_shapes=[
            pltpu.VMEM((row_count, tok_dev, width), jnp.bfloat16),
            pltpu.VMEM((tok_dev, cot_width), jnp.bfloat16),
            pltpu.VMEM((row_count, tok_dev, own), jnp.float32),
            pltpu.VMEM((row_count, ex_count, owned, own), jnp.float32),
            pltpu.VMEM((row_count, max(ex_count - 1, 1), owned, own), jnp.float32),
            pltpu.VMEM((others, owned, own), jnp.float32),
            pltpu.VMEM((row_count, owned, own), jnp.float32),
            pltpu.VMEM((others, owned, own), jnp.float32),
            pltpu.VMEM((row_count, own, own), jnp.bfloat16),
            pltpu.VMEM((owned, own), jnp.float32),
            dma((row_count,)),
            dma((others,)),
            dma((others,)),
            dma((row_count, max(ex_count - 1, 1))),
            dma((row_count, max(ex_count - 1, 1))),
            dma((others,)),
            dma((others,)),
            dma((others,)),
            dma((others,)),
        ],
        compiler_params=pltpu.CompilerParams(
            collective_id=0, has_side_effects=True, vmem_limit_bytes=60 * 1024 * 1024
        ),
        name="features_and_scores",
    )(
        hidden_acts,
        cotangent,
        lengths.reshape(1, -1),
        row_signs.reshape(1, -1),
        col_signs.reshape(1, -1),
        feat_row.reshape(1, -1),
        feat_col.reshape(1, -1),
        inverse_rows,
    )


def solution(mesh):
    placed = (
        P(("parts", "ex"), "rows"),
        P(("parts", "ex"), "rows"),
        P("parts"),
        P("rows"),
        P(),
        P(),
        P(),
        P("rows", None),
    )
    return jax.shard_map(
        local, mesh=mesh, in_specs=placed, out_specs=P(("parts", "ex"), "rows"), check_vma=False
    )
```

```python
import functools
import math

import jax
import jax.numpy as jnp
from jax import lax
from jax.experimental import pallas as pl
from jax.experimental.pallas import tpu as pltpu
from jax.sharding import PartitionSpec as P


def signs(first_bits, second_bits):
    odd = lax.population_count(first_bits & second_bits) & 1
    return (1 - 2 * odd).astype(jnp.float32).astype(jnp.bfloat16)


def sign_rows(first, count, step, picks):
    inner = lax.broadcasted_iota(jnp.int32, (step, picks.shape[1]), 0)
    table = signs(inner, picks)
    parts = [table * signs(jnp.zeros_like(picks) + (first + n * step), picks) for n in range(count)]
    return parts[0] if count == 1 else jnp.concatenate(parts, axis=0)


def loop(count, body):
    if count <= 4:
        for n in range(count):
            body(n)
    else:
        lax.fori_loop(0, count, lambda n, c: (body(n), c)[1], 0)


def when(cond, body):
    if isinstance(cond, bool):
        if cond:
            body()
    else:
        pl.when(cond)(body)


def kernel(
    row_count,
    ex_count,
    norm_scale,
    hid_ref,
    cot_ref,
    len_ref,
    rsign_ref,
    csign_ref,
    frow_ref,
    fcol_ref,
    inv_ref,
    out_ref,
    hid_all,
    cot_signed,
    right_buf,
    part_buf,
    ex_in,
    row_out,
    row_in,
    score_out,
    score_in,
    inv_buf,
    total_buf,
    inv_sem,
    hid_send,
    hid_recv,
    ex_send,
    ex_recv,
    row_send,
    row_recv,
    score_send,
    score_recv,
):
    row = lax.axis_index("rows")
    ex = lax.axis_index("ex")
    tok_dev, width = hid_ref.shape
    cot_width = cot_ref.shape[1]
    features = frow_ref.shape[1]
    own = features // row_count
    examples = len_ref.shape[1]
    chunk = min(own, 512)
    ex_steps = ex_count.bit_length() - 1

    def block_of(i):
        return lax.rem(row + 1 + i, row_count)

    def inv_copy(n):
        cols = pl.ds(pl.multiple_of(block_of(n) * own, 128), own)
        return pltpu.make_async_copy(inv_ref.at[:, cols], inv_buf.at[n], inv_sem.at[n])

    barrier = pltpu.get_barrier_semaphore()

    def greet(n):
        pl.semaphore_signal(
            barrier,
            inc=1,
            device_id={"rows": lax.rem(row + n + 1, row_count)},
            device_id_type=pl.DeviceIdType.MESH,
        )

    loop(row_count - 1, greet)

    def bit_of(step):
        return lax.rem(ex // (1 << step), 2)

    def partner_of(step):
        return ex + (1 - 2 * bit_of(step)) * (1 << step)

    for step in range(ex_steps):
        pl.semaphore_signal(
            barrier,
            inc=1,
            device_id={"ex": partner_of(step)},
            device_id_type=pl.DeviceIdType.MESH,
        )
    loop(row_count, lambda n: inv_copy(n).start())
    hid_all[row] = hid_ref[...] * rsign_ref[...].astype(jnp.float32).astype(jnp.bfloat16)
    if csign_ref.shape[1] == cot_width:
        col_sign = csign_ref[...]
    else:
        col_sign = csign_ref[:, pl.ds(pl.multiple_of(row * cot_width, 128), cot_width)]
    cot_signed[...] = cot_ref[...] * col_sign.astype(jnp.float32).astype(jnp.bfloat16)
    lens = jnp.broadcast_to(len_ref[...].astype(jnp.float32), (examples, examples))
    e_row = lax.broadcasted_iota(jnp.int32, (examples, examples), 0)
    e_col = lax.broadcasted_iota(jnp.int32, (examples, examples), 1)
    ends = jnp.sum(jnp.where(e_col <= e_row, lens, 0.0), axis=1, keepdims=True)
    starts = jnp.sum(jnp.where(e_col < e_row, lens, 0.0), axis=1, keepdims=True)
    spots = ex * tok_dev + lax.broadcasted_iota(jnp.int32, (examples, tok_dev), 1)
    spots = spots.astype(jnp.float32)
    member = jnp.where((spots >= starts) & (spots < ends), 1.0, 0.0).astype(jnp.bfloat16)
    pl.semaphore_wait(barrier, row_count - 1 + ex_steps)

    def hid_copy(n, incoming=False):
        to = lax.rem(row + n + 1, row_count)
        block = lax.rem(row - n - 1 + row_count, row_count) if incoming else row
        return pltpu.make_async_remote_copy(
            src_ref=hid_all.at[block],
            dst_ref=hid_all.at[block],
            send_sem=hid_send.at[n],
            recv_sem=hid_recv.at[n],
            device_id={"rows": to},
            device_id_type=pl.DeviceIdType.MESH,
        )

    loop(row_count - 1, lambda n: hid_copy(n).start())

    def picks_of(ref, i, c):
        at = pl.multiple_of(block_of(i) * own + c * chunk, 128)
        return ref[:, pl.ds(at, chunk)]

    inner = min(cot_width, 128)

    def right_side(i):
        def one(c):
            table = sign_rows(row * cot_width, cot_width // inner, inner, picks_of(fcol_ref, i, c))
            at = c * chunk if isinstance(c, int) else pl.multiple_of(c * chunk, 128)
            right_buf[i, :, pl.ds(at, chunk)] = jnp.dot(
                cot_signed[...], table, preferred_element_type=jnp.float32
            )

        loop(own // chunk, one)

    group = min(row_count, 4)

    def features_of(i):
        def one(c):
            picks = picks_of(frow_ref, i, c)

            def some(g, left):
                acts = jnp.concatenate([hid_all[g * group + n] for n in range(group)], axis=1)
                table = sign_rows(g * group * width, group, width, picks)
                return left + jnp.dot(acts, table, preferred_element_type=jnp.float32)

            left = jnp.zeros((tok_dev, chunk), jnp.float32)
            if row_count == group:
                left = some(0, left)
            else:
                left = lax.fori_loop(0, row_count // group, some, left)
            at = c * chunk if isinstance(c, int) else pl.multiple_of(c * chunk, 128)
            products = left * right_buf[i, :, pl.ds(at, chunk)]
            high = products.astype(jnp.bfloat16)
            rest = (products - high.astype(jnp.float32)).astype(jnp.bfloat16)
            sums = jnp.dot(member, high, preferred_element_type=jnp.float32)
            sums = sums + jnp.dot(member, rest, preferred_element_type=jnp.float32)
            part_buf[i, :, :, pl.ds(at, chunk)] = sums.reshape(ex_count, examples // ex_count, chunk)

        loop(own // chunk, one)

    def ex_copies(i, step):
        size = 1 << step
        first = ex_count - (ex_count >> step)
        copies = []
        for m in range(ex_count >> (step + 1)):
            away = lax.rem(ex, size) + (1 - bit_of(step)) * size + m * 2 * size
            slot = first + m
            copies.append(
                pltpu.make_async_remote_copy(
                    src_ref=part_buf.at[i, away],
                    dst_ref=ex_in.at[i, slot],
                    send_sem=ex_send.at[i, slot],
                    recv_sem=ex_recv.at[i, slot],
                    device_id={"ex": partner_of(step)},
                    device_id_type=pl.DeviceIdType.MESH,
                )
            )
        return copies

    def ex_start(i, step):
        for copy in ex_copies(i, step):
            copy.start()

    def ex_finish(i, step):
        size = 1 << step
        first = ex_count - (ex_count >> step)
        for m, copy in enumerate(ex_copies(i, step)):
            copy.wait_recv()
            mine = lax.rem(ex, 2 * size) + m * 2 * size
            part_buf[i, mine] = part_buf[i, mine] + ex_in[i, first + m]

    def row_copy(i):
        return pltpu.make_async_remote_copy(
            src_ref=row_out.at[i],
            dst_ref=row_in.at[i],
            send_sem=row_send.at[i],
            recv_sem=row_recv.at[i],
            device_id={"rows": block_of(i)},
            device_id_type=pl.DeviceIdType.MESH,
        )

    def stage(i, step):
        def work():
            if step > 0:
                ex_finish(i, step - 1)
            if step < ex_steps:
                ex_start(i, step)
            else:


                def send():
                    row_out[i] = part_buf[i, ex].astype(row_out.dtype)
                    row_copy(i).start()

                when(i < row_count - 1, send)

        return work

    loop(row_count, right_side)
    loop(row_count - 1, lambda n: hid_copy(n, True).wait_recv())

    def block_step(i):
        features_of(i)
        stage(i, 0)()
        for step in range(1, ex_steps + 1):
            when(i >= step, stage(i - step, step))

    loop(row_count, block_step)
    for late in range(1, ex_steps + 1):
        for step in range(late, ex_steps + 1):
            if row_count - 1 + late - step >= 0:
                stage(row_count - 1 + late - step, step)()

    total_buf[...] = part_buf[row_count - 1, ex]

    def add_row(n):
        row_copy(n).wait_recv()
        total_buf[...] = total_buf[...] + row_in[n].astype(jnp.float32)

    loop(row_count - 1, add_row)
    low = (total_buf[...] * norm_scale).astype(jnp.bfloat16)

    def score_copy(n):
        return pltpu.make_async_remote_copy(
            src_ref=score_out.at[n],
            dst_ref=score_in.at[n],
            send_sem=score_send.at[n],
            recv_sem=score_recv.at[n],
            device_id={"rows": block_of(n)},
            device_id_type=pl.DeviceIdType.MESH,
        )

    tile = min(own, 512)

    def score_block(n):
        inv_copy(n).wait()

        def one(j):
            at = j * tile if isinstance(j, int) else pl.multiple_of(j * tile, 128)
            got = jnp.dot(low, inv_buf[n, :, pl.ds(at, tile)], preferred_element_type=jnp.float32)

            def keep():
                total_buf[:, pl.ds(at, tile)] = got

            def give():
                score_out[n, :, pl.ds(at, tile)] = got.astype(score_out.dtype)

            when(n == row_count - 1, keep)
            when(n < row_count - 1, give)

        loop(own // tile, one)
        when(n < row_count - 1, lambda: score_copy(n).start())

    loop(row_count, score_block)
    def add_score(n):
        score_copy(n).wait_recv()
        total_buf[...] = total_buf[...] + score_in[n].astype(jnp.float32)

    loop(row_count - 1, add_score)
    out_ref[...] = total_buf[...].astype(out_ref.dtype)
    loop(row_count - 1, lambda n: hid_copy(n).wait_send())
    loop(row_count - 1, lambda n: score_copy(n).wait_send())
    loop(row_count - 1, lambda n: row_copy(n).wait_send())

    def ex_sent(i):
        for step in range(ex_steps):
            for copy in ex_copies(i, step):
                copy.wait_send()

    loop(row_count, ex_sent)


def local(hidden_acts, cotangent, lengths, row_signs, col_signs, feat_row, feat_col, inverse_rows):
    row_count = lax.axis_size("rows")
    ex_count = lax.axis_size("ex")
    tok_dev, width = hidden_acts.shape
    cot_width = cotangent.shape[1]
    features = feat_row.shape[0]
    examples = lengths.shape[0]
    own = features // row_count
    owned = examples // ex_count
    norm_scale = 1.0 / math.sqrt(width * row_count * col_signs.shape[0])
    if cot_width % 128 != 0:
        col_signs = lax.dynamic_slice(col_signs, (lax.axis_index("rows") * cot_width,), (cot_width,))
    vmem = pl.BlockSpec(memory_space=pltpu.VMEM)
    others = max(row_count - 1, 1)
    dma = pltpu.SemaphoreType.DMA
    return pl.pallas_call(
        functools.partial(kernel, row_count, ex_count, norm_scale),
        out_shape=jax.ShapeDtypeStruct((owned, own), jnp.bfloat16),
        in_specs=[vmem] * 7 + [pl.BlockSpec(memory_space=pl.ANY)],
        out_specs=vmem,
        scratch_shapes=[
            pltpu.VMEM((row_count, tok_dev, width), jnp.bfloat16),
            pltpu.VMEM((tok_dev, cot_width), jnp.bfloat16),
            pltpu.VMEM((row_count, tok_dev, own), jnp.float32),
            pltpu.VMEM((row_count, ex_count, owned, own), jnp.float32),
            pltpu.VMEM((row_count, max(ex_count - 1, 1), owned, own), jnp.float32),
            pltpu.VMEM((others, owned, own), jnp.bfloat16),
            pltpu.VMEM((others, owned, own), jnp.bfloat16),
            pltpu.VMEM((others, owned, own), jnp.bfloat16),
            pltpu.VMEM((others, owned, own), jnp.bfloat16),
            pltpu.VMEM((row_count, own, own), jnp.bfloat16),
            pltpu.VMEM((owned, own), jnp.float32),
            dma((row_count,)),
            dma((others,)),
            dma((others,)),
            dma((row_count, max(ex_count - 1, 1))),
            dma((row_count, max(ex_count - 1, 1))),
            dma((others,)),
            dma((others,)),
            dma((others,)),
            dma((others,)),
        ],
        compiler_params=pltpu.CompilerParams(
            collective_id=0, has_side_effects=True, vmem_limit_bytes=60 * 1024 * 1024
        ),
        name="features_and_scores",
    )(
        hidden_acts,
        cotangent,
        lengths.reshape(1, -1),
        row_signs.reshape(1, -1),
        col_signs.reshape(1, -1),
        feat_row.reshape(1, -1),
        feat_col.reshape(1, -1),
        inverse_rows,
    )


def solution(mesh):
    placed = (
        P(("parts", "ex"), "rows"),
        P(("parts", "ex"), "rows"),
        P("parts"),
        P("rows"),
        P(),
        P(),
        P(),
        P("rows", None),
    )
    return jax.shard_map(
        local, mesh=mesh, in_specs=placed, out_specs=P(("parts", "ex"), "rows"), check_vma=False
    )
```

```python
import functools
import math

import jax
import jax.numpy as jnp
from jax import lax
from jax.experimental import pallas as pl
from jax.experimental.pallas import tpu as pltpu
from jax.sharding import PartitionSpec as P


def signs(first_bits, second_bits):
    odd = lax.population_count(first_bits & second_bits) & 1
    return (1 - 2 * odd).astype(jnp.float32).astype(jnp.bfloat16)


def sign_rows(first, count, step, picks):
    inner = lax.broadcasted_iota(jnp.int32, (step, picks.shape[1]), 0)
    table = signs(inner, picks)
    parts = [table * signs(jnp.zeros_like(picks) + (first + n * step), picks) for n in range(count)]
    return parts[0] if count == 1 else jnp.concatenate(parts, axis=0)


def loop(count, body):
    if count <= 4:
        for n in range(count):
            body(n)
    else:
        lax.fori_loop(0, count, lambda n, c: (body(n), c)[1], 0)


def when(cond, body):
    if isinstance(cond, bool):
        if cond:
            body()
    else:
        pl.when(cond)(body)


def kernel(
    row_count,
    ex_count,
    norm_scale,
    hid_ref,
    cot_ref,
    len_ref,
    rsign_ref,
    csign_ref,
    frow_ref,
    fcol_ref,
    inv_ref,
    out_ref,
    hid_all,
    cot_signed,
    right_buf,
    part_buf,
    ex_in,
    row_out,
    row_in,
    score_out,
    score_in,
    inv_buf,
    total_buf,
    inv_sem,
    hid_send,
    hid_recv,
    ex_send,
    ex_recv,
    row_send,
    row_recv,
    score_send,
    score_recv,
):
    row = lax.axis_index("rows")
    ex = lax.axis_index("ex")
    tok_dev, width = hid_ref.shape
    cot_width = cot_ref.shape[1]
    features = frow_ref.shape[1]
    own = features // row_count
    examples = len_ref.shape[1]
    chunk = min(own, 512)
    ex_steps = ex_count.bit_length() - 1

    def block_of(i):
        return lax.rem(row + 1 + i, row_count)

    def inv_copy(n):
        cols = pl.ds(pl.multiple_of(block_of(n) * own, 128), own)
        return pltpu.make_async_copy(inv_ref.at[:, cols], inv_buf.at[n], inv_sem.at[n])

    barrier = pltpu.get_barrier_semaphore()

    def greet(n):
        pl.semaphore_signal(
            barrier,
            inc=1,
            device_id={"rows": lax.rem(row + n + 1, row_count)},
            device_id_type=pl.DeviceIdType.MESH,
        )

    loop(row_count - 1, greet)

    def bit_of(step):
        return lax.rem(ex // (1 << step), 2)

    def partner_of(step):
        return ex + (1 - 2 * bit_of(step)) * (1 << step)

    for step in range(ex_steps):
        pl.semaphore_signal(
            barrier,
            inc=1,
            device_id={"ex": partner_of(step)},
            device_id_type=pl.DeviceIdType.MESH,
        )
    loop(row_count, lambda n: inv_copy(n).start())
    hid_all[row] = hid_ref[...] * rsign_ref[...].astype(jnp.float32).astype(jnp.bfloat16)
    if csign_ref.shape[1] == cot_width:
        col_sign = csign_ref[...]
    else:
        col_sign = csign_ref[:, pl.ds(pl.multiple_of(row * cot_width, 128), cot_width)]
    cot_signed[...] = cot_ref[...] * col_sign.astype(jnp.float32).astype(jnp.bfloat16)
    lens = jnp.broadcast_to(len_ref[...].astype(jnp.float32), (examples, examples))
    e_row = lax.broadcasted_iota(jnp.int32, (examples, examples), 0)
    e_col = lax.broadcasted_iota(jnp.int32, (examples, examples), 1)
    ends = jnp.sum(jnp.where(e_col <= e_row, lens, 0.0), axis=1, keepdims=True)
    starts = jnp.sum(jnp.where(e_col < e_row, lens, 0.0), axis=1, keepdims=True)
    spots = ex * tok_dev + lax.broadcasted_iota(jnp.int32, (examples, tok_dev), 1)
    spots = spots.astype(jnp.float32)
    member = jnp.where((spots >= starts) & (spots < ends), 1.0, 0.0).astype(jnp.bfloat16)
    pl.semaphore_wait(barrier, row_count - 1 + ex_steps)

    def hid_copy(n, incoming=False):
        to = lax.rem(row + n + 1, row_count)
        block = lax.rem(row - n - 1 + row_count, row_count) if incoming else row
        return pltpu.make_async_remote_copy(
            src_ref=hid_all.at[block],
            dst_ref=hid_all.at[block],
            send_sem=hid_send.at[n],
            recv_sem=hid_recv.at[n],
            device_id={"rows": to},
            device_id_type=pl.DeviceIdType.MESH,
        )

    loop(row_count - 1, lambda n: hid_copy(n).start())

    def picks_of(ref, i, c):
        at = pl.multiple_of(block_of(i) * own + c * chunk, 128)
        return ref[:, pl.ds(at, chunk)]

    inner = min(cot_width, 128)

    def right_side(i):
        def one(c):
            table = sign_rows(row * cot_width, cot_width // inner, inner, picks_of(fcol_ref, i, c))
            at = c * chunk if isinstance(c, int) else pl.multiple_of(c * chunk, 128)
            right_buf[i, :, pl.ds(at, chunk)] = jnp.dot(
                cot_signed[...], table, preferred_element_type=jnp.float32
            )

        loop(own // chunk, one)

    group = min(row_count, 4)

    def features_of(i):
        def one(c):
            picks = picks_of(frow_ref, i, c)

            def some(g, left):
                acts = jnp.concatenate([hid_all[g * group + n] for n in range(group)], axis=1)
                table = sign_rows(g * group * width, group, width, picks)
                return left + jnp.dot(acts, table, preferred_element_type=jnp.float32)

            left = jnp.zeros((tok_dev, chunk), jnp.float32)
            if row_count == group:
                left = some(0, left)
            else:
                left = lax.fori_loop(0, row_count // group, some, left)
            at = c * chunk if isinstance(c, int) else pl.multiple_of(c * chunk, 128)
            products = left * right_buf[i, :, pl.ds(at, chunk)]
            high = products.astype(jnp.bfloat16)
            rest = (products - high.astype(jnp.float32)).astype(jnp.bfloat16)
            sums = jnp.dot(member, high, preferred_element_type=jnp.float32)
            sums = sums + jnp.dot(member, rest, preferred_element_type=jnp.float32)
            part_buf[i, :, :, pl.ds(at, chunk)] = sums.reshape(ex_count, examples // ex_count, chunk)

        loop(own // chunk, one)

    def ex_copies(i, step):
        size = 1 << step
        first = ex_count - (ex_count >> step)
        copies = []
        for m in range(ex_count >> (step + 1)):
            away = lax.rem(ex, size) + (1 - bit_of(step)) * size + m * 2 * size
            slot = first + m
            copies.append(
                pltpu.make_async_remote_copy(
                    src_ref=part_buf.at[i, away],
                    dst_ref=ex_in.at[i, slot],
                    send_sem=ex_send.at[i, slot],
                    recv_sem=ex_recv.at[i, slot],
                    device_id={"ex": partner_of(step)},
                    device_id_type=pl.DeviceIdType.MESH,
                )
            )
        return copies

    def ex_start(i, step):
        for copy in ex_copies(i, step):
            copy.start()

    def ex_finish(i, step):
        size = 1 << step
        first = ex_count - (ex_count >> step)
        for m, copy in enumerate(ex_copies(i, step)):
            copy.wait_recv()
            mine = lax.rem(ex, 2 * size) + m * 2 * size
            part_buf[i, mine] = part_buf[i, mine] + ex_in[i, first + m]

    def row_copy(i):
        return pltpu.make_async_remote_copy(
            src_ref=row_out.at[i],
            dst_ref=row_in.at[i],
            send_sem=row_send.at[i],
            recv_sem=row_recv.at[i],
            device_id={"rows": block_of(i)},
            device_id_type=pl.DeviceIdType.MESH,
        )

    def stage(i, step):
        def work():
            if step > 0:
                ex_finish(i, step - 1)
            if step < ex_steps:
                ex_start(i, step)
            else:


                def send():
                    row_out[i] = part_buf[i, ex].astype(row_out.dtype)
                    row_copy(i).start()

                when(i < row_count - 1, send)

        return work

    loop(row_count, right_side)
    loop(row_count - 1, lambda n: hid_copy(n, True).wait_recv())

    def block_step(i):
        for step in range(ex_steps, 0, -1):
            when(i >= step, stage(i - step, step))
        features_of(i)
        stage(i, 0)()

    loop(row_count, block_step)
    for late in range(1, ex_steps + 1):
        for step in range(late, ex_steps + 1):
            if row_count - 1 + late - step >= 0:
                stage(row_count - 1 + late - step, step)()

    total_buf[...] = part_buf[row_count - 1, ex]

    def add_row(n):
        row_copy(n).wait_recv()
        total_buf[...] = total_buf[...] + row_in[n].astype(jnp.float32)

    loop(row_count - 1, add_row)
    low = (total_buf[...] * norm_scale).astype(jnp.bfloat16)

    def score_copy(n):
        return pltpu.make_async_remote_copy(
            src_ref=score_out.at[n],
            dst_ref=score_in.at[n],
            send_sem=score_send.at[n],
            recv_sem=score_recv.at[n],
            device_id={"rows": block_of(n)},
            device_id_type=pl.DeviceIdType.MESH,
        )

    tile = min(own, 512)

    def score_block(n):
        inv_copy(n).wait()

        def one(j):
            at = j * tile if isinstance(j, int) else pl.multiple_of(j * tile, 128)
            got = jnp.dot(low, inv_buf[n, :, pl.ds(at, tile)], preferred_element_type=jnp.float32)

            def keep():
                total_buf[:, pl.ds(at, tile)] = got

            def give():
                score_out[n, :, pl.ds(at, tile)] = got.astype(score_out.dtype)

            when(n == row_count - 1, keep)
            when(n < row_count - 1, give)

        loop(own // tile, one)
        when(n < row_count - 1, lambda: score_copy(n).start())

    loop(row_count, score_block)
    def add_score(n):
        score_copy(n).wait_recv()
        total_buf[...] = total_buf[...] + score_in[n].astype(jnp.float32)

    loop(row_count - 1, add_score)
    out_ref[...] = total_buf[...].astype(out_ref.dtype)
    loop(row_count - 1, lambda n: hid_copy(n).wait_send())
    loop(row_count - 1, lambda n: score_copy(n).wait_send())
    loop(row_count - 1, lambda n: row_copy(n).wait_send())

    def ex_sent(i):
        for step in range(ex_steps):
            for copy in ex_copies(i, step):
                copy.wait_send()

    loop(row_count, ex_sent)


def local(hidden_acts, cotangent, lengths, row_signs, col_signs, feat_row, feat_col, inverse_rows):
    row_count = lax.axis_size("rows")
    ex_count = lax.axis_size("ex")
    tok_dev, width = hidden_acts.shape
    cot_width = cotangent.shape[1]
    features = feat_row.shape[0]
    examples = lengths.shape[0]
    own = features // row_count
    owned = examples // ex_count
    norm_scale = 1.0 / math.sqrt(width * row_count * col_signs.shape[0])
    if cot_width % 128 != 0:
        col_signs = lax.dynamic_slice(col_signs, (lax.axis_index("rows") * cot_width,), (cot_width,))
    vmem = pl.BlockSpec(memory_space=pltpu.VMEM)
    others = max(row_count - 1, 1)
    dma = pltpu.SemaphoreType.DMA
    return pl.pallas_call(
        functools.partial(kernel, row_count, ex_count, norm_scale),
        out_shape=jax.ShapeDtypeStruct((owned, own), jnp.bfloat16),
        in_specs=[vmem] * 7 + [pl.BlockSpec(memory_space=pl.ANY)],
        out_specs=vmem,
        scratch_shapes=[
            pltpu.VMEM((row_count, tok_dev, width), jnp.bfloat16),
            pltpu.VMEM((tok_dev, cot_width), jnp.bfloat16),
            pltpu.VMEM((row_count, tok_dev, own), jnp.float32),
            pltpu.VMEM((row_count, ex_count, owned, own), jnp.float32),
            pltpu.VMEM((row_count, max(ex_count - 1, 1), owned, own), jnp.float32),
            pltpu.VMEM((others, owned, own), jnp.bfloat16),
            pltpu.VMEM((others, owned, own), jnp.bfloat16),
            pltpu.VMEM((others, owned, own), jnp.bfloat16),
            pltpu.VMEM((others, owned, own), jnp.bfloat16),
            pltpu.VMEM((row_count, own, own), jnp.bfloat16),
            pltpu.VMEM((owned, own), jnp.float32),
            dma((row_count,)),
            dma((others,)),
            dma((others,)),
            dma((row_count, max(ex_count - 1, 1))),
            dma((row_count, max(ex_count - 1, 1))),
            dma((others,)),
            dma((others,)),
            dma((others,)),
            dma((others,)),
        ],
        compiler_params=pltpu.CompilerParams(
            collective_id=0, has_side_effects=True, vmem_limit_bytes=60 * 1024 * 1024
        ),
        name="features_and_scores",
    )(
        hidden_acts,
        cotangent,
        lengths.reshape(1, -1),
        row_signs.reshape(1, -1),
        col_signs.reshape(1, -1),
        feat_row.reshape(1, -1),
        feat_col.reshape(1, -1),
        inverse_rows,
    )


def solution(mesh):
    placed = (
        P(("parts", "ex"), "rows"),
        P(("parts", "ex"), "rows"),
        P("parts"),
        P("rows"),
        P(),
        P(),
        P(),
        P("rows", None),
    )
    return jax.shard_map(
        local, mesh=mesh, in_specs=placed, out_specs=P(("parts", "ex"), "rows"), check_vma=False
    )
```
